256 devices in a mesh: tm: 16 (over z, core), tok: 16 (over x, y).
Axes of the slice: x: 4, y: 4, z: 8, core: 2. Of those that a mesh axis runs over, the one named last changes fastest.
Arguments:
- queries: bfloat16 [32, 2048, 1024], P('tm', 'tok'), may hold values from -6 to 6
- keys: bfloat16 [32, 2048, 1024], P('tm', 'tok'), may hold values from -6 to 6
- values: bfloat16 [32, 2048, 1024], P('tm', 'tok'), may hold values from -6 to 6
- epi_dev: int32 [32, 6], replicated, may hold values from 0 to 15, all different within a row; in each aligned block of 2 rows (0 to 1, 2 to 3, ...) at most 2 rows name the same one
- epi_frame: int32 [32, 6], replicated, may hold values from 0 to 1
- epi_block: int32 [32, 6], replicated, may hold values from 0 to 15
- valid: int32 [32, 6], replicated, may hold values 0 or 1
- ref_local: int32 [4], replicated, may hold values from 0 to 7
Outputs:
- attended: bfloat16 [32, 2048, 1024], P('tm', 'tok')
The draws below stay inside these ranges and needn't reach their ends.
Inputs may be any that keep to these rules, and one draw needn't show every extreme that they name: `epi_dev`: the 6 values of one frame differ. Among the frames of one index of tm (aligned blocks of 2 frames), no value is named by more than 2 entries, a bound that some block reaches.
All inputs are finite; a program needn't handle non-finite values.
Results may differ from the reference program's by a relative error of at most 0.0032.
Values may be sent and summed in bfloat16 or wider, within the bound.
A program may use at most 128 MiB of HBM per device.

```python
import math
import jax
import jax.numpy as jnp
import numpy as np
from jax import lax

HEADS = 16
HEAD_DIM = 64
BLOCK = 128
FRAMES_DEV = 2
ENTRIES = 6
CAPACITY = 2
SPAN = 4
WIDTH = 1024
FRAMES = 32
TOKENS = 2048
GROUPS = 4
N_TM = 16
N_TOK = 16


def drawn_pair(key):
    key_q, key_k = jax.random.split(jax.random.fold_in(key, 4242), 2)
    full_shape = (FRAMES, TOKENS, WIDTH)
    query_table = jnp.clip(1.6 * jax.random.normal(key_q, full_shape, jnp.float32), -6.0, 6.0)
    key_table = jnp.clip(1.6 * jax.random.normal(key_k, full_shape, jnp.float32), -6.0, 6.0)
    return (query_table, key_table)


def draw_queries(key, part):
    return drawn_pair(key)[0].astype(jnp.bfloat16)


def draw_keys(key, part):
    return drawn_pair(key)[1].astype(jnp.bfloat16)


def touch_ends(entries, stream_key, low, top_value):
    index_at = [jax.random.randint(jax.random.fold_in(stream_key, axis), (), 0, length) for axis, length in enumerate(entries.shape)]
    widest = entries.shape.index(max(entries.shape))
    neighbour = index_at[:widest] + [(index_at[widest] + 1) % entries.shape[widest]] + index_at[widest + 1:]
    return entries.at[tuple(index_at)].set(low).at[tuple(neighbour)].set(top_value)


def block_levels(key, dims, cuts, least, largest):
    def one(position, parts):
        heights = jax.random.uniform(jax.random.fold_in(jax.random.fold_in(key, 6), position), (parts,), jnp.float32, least / len(cuts), largest / len(cuts))
        return jnp.repeat(jnp.exp(heights), dims[position] // parts).reshape((-1,) + (1,) * (len(dims) - position - 1))

    factor_of = one(*cuts[0])
    for cut in cuts[1:]:
        factor_of = factor_of * one(*cut)
    return factor_of


def deal_out(own_key, own, number, rows, count, top, most, skew):
    ranking = jax.random.permutation(own_key, count)
    packed, ordinary = load_shares(count, rows * top, most, skew, True), load_shares(count, rows * top, most, skew, False)
    places = jnp.arange(count)

    def named(tallies, turn):
        used = int((tallies > 0).sum())
        fixed = max(1, used // 4)
        moved = fixed + (places - fixed + turn * (used - fixed)) % max(1, count - fixed)
        return jnp.zeros((count,), jnp.int32).at[ranking[jnp.where(places < fixed, places, moved)]].set(jnp.asarray(tallies, jnp.int32))

    tallies = jnp.where(number % 4 == 0, named(packed, number // 4), named(ordinary, number - number // 4 - 1))
    mixed = jax.random.permutation(jax.random.fold_in(own, 3), count)
    donor, receiver = mixed[0:count // 2 * 2:2], mixed[1:count // 2 * 2:2]
    room = jnp.minimum(tallies[donor] - 1, most - tallies[receiver]) // 2
    room = jnp.where((donor == ranking[0]) | (receiver == ranking[0]) | (tallies[receiver] == 0), 0, jnp.maximum(room, 0))
    moved = jax.random.randint(jax.random.fold_in(own, 4), (count // 2,), 0, 1 << 20) % (room + 1)
    tallies = tallies.at[donor].add(-moved).at[receiver].add(moved)
    labels = jnp.searchsorted(jnp.cumsum(tallies), jnp.arange(rows * top), side="right").astype(jnp.int32)
    listing = labels.reshape(top, rows).T
    listing = listing[jax.random.permutation(jax.random.fold_in(own, 1), rows)]
    turn = jax.random.randint(jax.random.fold_in(own, 2), (rows, 1), 0, top)
    return jnp.take_along_axis(listing, (jnp.arange(top)[None, :] + turn) % top, axis=1)


def load_shares(amount, total, most, slope, full):
    portions = [(1 << 20) // math.isqrt(rank ** slope) + 1 for rank in range(1, amount + 1)]
    largest = most if full else min(most, max(-(-total // amount), total * portions[0] // sum(portions)))
    least = 1 if total - largest >= amount - 1 else 0
    given, spare = [largest] + [least] * (amount - 1), total - largest - least * (amount - 1)
    while spare > 0:
        free = [i for i in range(1, amount) if given[i] < largest] or [i for i in range(1, amount) if given[i] < most]
        whole, remaining = sum([portions[i] for i in free]), spare
        for i in free:
            more = min(most - given[i], max(1, remaining * portions[i] // whole), spare)
            given[i] = given[i] + more
            spare = spare - more
    return np.array(given)


def bell_draw(rng, dims, spread, most, shards=(), kind=jnp.bfloat16):
    values = jax.random.normal(rng, dims, jnp.float32) * spread
    if len(shards) > 0:
        values = block_levels(rng, dims, shards, -0.22, 0.18) * values
    return jnp.clip(values, min=-most, max=most).astype(kind)


def setup_inputs(seed: int = 0) -> dict:
    key_of = jax.random.split(jax.random.key(seed), 9)
    queries = draw_queries(jax.random.fold_in(key_of[8], 71), 0)
    keys = draw_keys(jax.random.fold_in(key_of[8], 71), 0)
    values = bell_draw(key_of[2], (FRAMES, TOKENS, WIDTH), 1.0, 6.0, ((0, 16), (1, 16)))
    epi_dev_keys = jax.random.split(jax.random.fold_in(key_of[3], 1), FRAMES // FRAMES_DEV)
    epi_dev_turns = jax.random.permutation(jax.random.fold_in(key_of[3], 3), FRAMES // FRAMES_DEV)
    epi_dev = jax.vmap(lambda own, number: deal_out(jax.random.fold_in(key_of[3], 2), own, number, FRAMES_DEV, N_TM, ENTRIES, CAPACITY, 2))(epi_dev_keys, epi_dev_turns).reshape((FRAMES, ENTRIES))
    epi_frame = touch_ends(jax.random.randint(key_of[4], (FRAMES, ENTRIES), 0, FRAMES_DEV), jax.random.fold_in(key_of[4], 1), 0, FRAMES_DEV - 1).astype(jnp.int32)
    epi_block = touch_ends(jax.random.randint(key_of[5], (FRAMES, ENTRIES), 0, N_TOK), jax.random.fold_in(key_of[5], 1), 0, N_TOK - 1).astype(jnp.int32)
    valid = touch_ends((jax.random.randint(key_of[6], (FRAMES, ENTRIES), 0, 4) < 3).astype(jnp.int32), jax.random.fold_in(key_of[6], 1), 0, 1)
    ref_local = touch_ends(jax.random.randint(key_of[7], (GROUPS,), 0, SPAN * FRAMES_DEV), jax.random.fold_in(key_of[7], 1), 0, (SPAN * FRAMES_DEV) - 1).astype(jnp.int32)
    return dict(queries=queries, keys=keys, values=values, epi_dev=epi_dev, epi_frame=epi_frame, epi_block=epi_block, valid=valid, ref_local=ref_local)


def reference(queries, keys, values, epi_dev, epi_frame, epi_block, valid, ref_local):
    head_q = queries.reshape(FRAMES, TOKENS, HEADS, HEAD_DIM)
    head_k = keys.reshape(FRAMES, TOKENS, HEADS, HEAD_DIM)
    head_v = values.reshape(FRAMES, TOKENS, HEADS, HEAD_DIM)
    source = (epi_dev * FRAMES_DEV + epi_frame).astype(jnp.int32)
    group_frames = SPAN * FRAMES_DEV
    score_scale = HEAD_DIM ** -0.5
    block_rows = math.gcd(TOKENS, 512)
    zero_index = jnp.zeros((), jnp.int32)

    def one_frame(frame_index):
        group_index = (frame_index // group_frames).astype(jnp.int32)
        ref_frame = (group_index * group_frames + ref_local[group_index]).astype(jnp.int32)
        key_parts = [head_k[frame_index], head_k[ref_frame]]
        value_parts = [head_v[frame_index], head_v[ref_frame]]
        for entry in range(ENTRIES):
            corner = (source[frame_index, entry].astype(jnp.int32), (epi_block[frame_index, entry] * BLOCK).astype(jnp.int32), zero_index, zero_index)
            key_parts.append(lax.dynamic_slice(head_k, corner, (1, BLOCK, HEADS, HEAD_DIM))[0])
            value_parts.append(lax.dynamic_slice(head_v, corner, (1, BLOCK, HEADS, HEAD_DIM))[0])
        key_set = jnp.concatenate(key_parts, 0).astype(jnp.float32)
        value_set = jnp.concatenate(value_parts, 0).astype(jnp.float32)
        live_mask = jnp.concatenate([jnp.ones((2 * TOKENS,), jnp.float32), jnp.repeat(valid[frame_index].astype(jnp.float32), BLOCK)])
        query_blocks = head_q[frame_index].astype(jnp.float32).reshape(TOKENS // block_rows, block_rows, HEADS, HEAD_DIM)

        def per_block(query_block):
            scores = jnp.einsum("qhd,khd->hqk", query_block, key_set) * score_scale
            scores = jnp.where(live_mask > 0, scores, -1e30)
            row_max = jnp.max(scores, axis=-1, keepdims=True)
            weights = jnp.exp(scores - row_max) * live_mask
            weight_sum = jnp.sum(weights, axis=-1)
            probs = lax.optimization_barrier(weights.astype(jnp.bfloat16)).astype(jnp.float32)
            attended = jnp.einsum("hqk,khd->qhd", probs, value_set) / jnp.transpose(weight_sum)[:, :, None]
            return attended.astype(jnp.bfloat16).reshape(block_rows, WIDTH)

        return lax.map(per_block, query_blocks).reshape(TOKENS, WIDTH)

    return lax.map(one_frame, jnp.arange(FRAMES, dtype=jnp.int32))
```

```python
import functools
import math

import jax
import jax.numpy as jnp
from jax import lax
from jax.experimental import pallas as pl
from jax.experimental.pallas import tpu as pltpu
from jax.sharding import PartitionSpec as P

HEADS = 16
HEAD_DIM = 64
BLOCK = 128
FRAMES_DEV = 2
ENTRIES = 6
SPAN = 4
TOKENS = 2048
N = 16
TILE = 1024
TILES = TOKENS // TILE
ROWS = HEAD_DIM + 16
EPI = ENTRIES * BLOCK
QK_SCALE = HEAD_DIM**-0.5 * math.log2(math.e)
MESH = pl.DeviceIdType.MESH
BF16 = jnp.bfloat16
F32 = jnp.float32


def low_halves(a, b):
    return jnp.concatenate([a[:, :HEAD_DIM], b[:, :HEAD_DIM]], axis=1)


def high_halves(a, b):
    return jnp.concatenate([a[:, HEAD_DIM:], b[:, HEAD_DIM:]], axis=1)


def kernel(
    q_ref, k_ref, v_ref, dev_ref, frame_ref, block_ref, valid_ref, local_ref, o_ref,
    s_kv, s_q, r_kv, r_q, s_epi, r_epi, cands, cross, r_cross, k_own, v_own, k_epi, v_epi,
    q_two, acc, top, scores, s_out, r_out, send_table, recv_table,
    sem_kv, sem_q, sem_epi, sem_out, sem_ref,
):
    tm, tok = lax.axis_index("tm"), lax.axis_index("tok")
    core, pair = lax.rem(tm, 2), lax.rem(tm // 2, 2)
    partner, across = tm + 1 - 2 * core, tm + 2 - 4 * pair
    group = tm // SPAN

    def other(me, step):
        return lax.rem(me + step, N)

    def rest(fn):
        lax.fori_loop(1, N, lambda step, _: (fn(step), 0)[1], 0)

    def copy(src, dst, sems, sent, got, axis, to):
        return pltpu.make_async_remote_copy(
            src_ref=src, dst_ref=dst, send_sem=sems.at[0, sent], recv_sem=sems.at[1, got],
            device_id={axis: to}, device_id_type=MESH,
        )

    barrier = pltpu.get_barrier_semaphore()

    def greet(step):
        pl.semaphore_signal(barrier, inc=1, device_id={"tok": other(tok, step)}, device_id_type=MESH)
        pl.semaphore_signal(barrier, inc=1, device_id={"tm": other(tm, step)}, device_id_type=MESH)

    rest(greet)

    for j in range(HEADS // 2):
        lanes = slice(j * 128, (j + 1) * 128)
        for f in range(FRAMES_DEV):
            k, v = k_ref[f, :, lanes], v_ref[f, :, lanes]
            s_kv[(2 * j) * 2 + f] = low_halves(k, v)
            s_kv[(2 * j + 1) * 2 + f] = high_halves(k, v)
        q0, q1 = q_ref[0, :, lanes], q_ref[1, :, lanes]
        s_q[2 * j] = low_halves(q0, q1)
        s_q[2 * j + 1] = high_halves(q0, q1)

    pl.semaphore_wait(barrier, 2 * (N - 1))

    def kv_copy(sent, got, to):
        return copy(s_kv.at[pl.ds(to * 2, 2)], r_kv.at[pl.ds(got * 2, 2)], sem_kv, sent, got, "tok", to)

    def q_copy(sent, got, to):
        return copy(s_q.at[to], r_q.at[got], sem_q, sent, got, "tok", to)

    rest(lambda step: kv_copy(step, tok, other(tok, step)).start())
    rest(lambda step: q_copy(step, tok, other(tok, step)).start())
    r_kv[pl.ds(tok * 2, 2)] = s_kv[pl.ds(tok * 2, 2)]
    r_q[tok] = s_q[tok]

    def fill_send(d, _):
        count, first, second = jnp.int32(0), jnp.int32(0), jnp.int32(0)
        for f in range(FRAMES_DEV):
            for e in range(ENTRIES):
                row = d * FRAMES_DEV + f
                hit = jnp.where(dev_ref[row, e] == tm, 1, 0)
                place = block_ref[row, e] * 2 + frame_ref[row, e]
                first = jnp.where((hit == 1) & (count == 0), place, first)
                second = jnp.where((hit == 1) & (count == 1), place, second)
                count = count + hit
        send_table[d * 2] = first
        send_table[d * 2 + 1] = second
        return 0

    lax.fori_loop(0, N, fill_send, 0)
    names = [dev_ref[tm * FRAMES_DEV + f, e] for f in range(FRAMES_DEV) for e in range(ENTRIES)]
    for i, name in enumerate(names):
        slot = jnp.int32(0)
        for before in names[:i]:
            slot = slot + jnp.where(before == name, 1, 0)
        recv_table[i] = name * 2 + jnp.minimum(slot, 1)

    rest(lambda step: kv_copy(step, other(tok, step), other(tok, step)).wait_recv())

    local = local_ref[group]
    owner_core, owner_pair, ref_bit = lax.rem(local // 2, 2), local // 4, lax.rem(local, 2)
    for b in range(N):
        cands[core, b] = r_kv[b * 2 + ref_bit]
    swap = copy(cands.at[core], cands.at[core], sem_ref, 0, 0, "tm", partner)
    swap.start()

    def fill_epi(i, _):
        s_epi[i] = r_kv[send_table[i]]
        return 0

    lax.fori_loop(0, 2 * N, fill_epi, 0, unroll=4)

    def ones_rows(ref, width):
        ref[0:16, :] = jnp.ones((16, width), BF16)

    for f in range(3):
        ones_rows(v_own.at[f], TOKENS)

    def build_own(b, f):
        kv = r_kv[b * 2 + f]
        at = pl.ds(pl.multiple_of(b * BLOCK, BLOCK), BLOCK)
        k_own[f, at, :] = low_halves(kv, kv)
        v_own[f, 16:, at] = kv.T[HEAD_DIM:]

    def build_frame(f):
        lax.fori_loop(0, N, lambda b, _: (build_own(b, f), 0)[1], 0, unroll=4)

    build_frame(0)
    swap.wait_recv()
    half = N // 2
    cross[...] = cands[owner_core, pl.ds(core * half, half)]
    hop = copy(cross, r_cross.at[pl.ds(core * half, half)], sem_ref, 1, 1, "tm", across)
    hop.start()

    def epi_copy(sent, got, to):
        return copy(s_epi.at[pl.ds(to * 2, 2)], r_epi.at[pl.ds(got * 2, 2)], sem_epi, sent, got, "tm", to)

    rest(lambda step: epi_copy(step, tm, other(tm, step)).start())
    r_epi[pl.ds(tm * 2, 2)] = s_epi[pl.ds(tm * 2, 2)]
    build_frame(1)

    rest(lambda step: q_copy(step, other(tok, step), other(tok, step)).wait_recv())

    def build_q(b, _):
        x = r_q[b].astype(F32) * QK_SCALE
        hi = x.astype(BF16)
        lo = (x - hi.astype(F32)).astype(BF16)
        at = pl.ds(pl.multiple_of(b * BLOCK, BLOCK), BLOCK)
        q_two[0, at, :] = low_halves(hi, lo)
        q_two[1, at, :] = high_halves(hi, lo)
        return 0

    lax.fori_loop(0, N, build_q, 0, unroll=4)

    acc[...] = jnp.zeros_like(acc)
    top[...] = jnp.full_like(top, -1e30)

    def attend(f, tile, keys, values):
        rows = pl.ds(pl.multiple_of(tile * TILE, TILE), TILE)
        length = keys.shape[0]
        s = lax.dot_general(keys[...], q_two[f, rows, :], (((1,), (1,)), ((), ())), preferred_element_type=F32)
        scores[0:length, :] = s
        peak = jnp.max(jnp.max(s.reshape(length // 8, 8, TILE), axis=0), axis=0, keepdims=True)
        old = top[f, tile]
        new = jnp.maximum(old, jnp.broadcast_to(peak, (8, TILE)))
        top[f, tile] = new
        kept = acc[f, tile] * jnp.exp2(old - new)[:1]
        probs = jnp.exp2(scores[0:length, :] - new[:1]).astype(BF16)
        acc[f, tile] = kept + jnp.dot(values[...], probs, preferred_element_type=F32)

    swap_back = copy(
        r_cross.at[pl.ds(core * half, half)], r_cross.at[pl.ds(core * half, half)], sem_ref, 2, 2, "tm", partner
    )
    swap_in = copy(
        r_cross.at[pl.ds((1 - core) * half, half)], r_cross.at[pl.ds((1 - core) * half, half)],
        sem_ref, 2, 2, "tm", partner,
    )
    phase = FRAMES_DEV * TILES

    def long_step(n, _):
        @pl.when(n == TILES)
        def _():
            hop.wait_recv()
            swap_back.start()

        @pl.when(n == phase)
        def _():
            swap_in.wait_recv()
            here = owner_pair == pair

            def build_ref(b, _):
                kv = jnp.where(here, cands[owner_core, b], r_cross[b])
                at = pl.ds(pl.multiple_of(b * BLOCK, BLOCK), BLOCK)
                k_own[2, at, :] = low_halves(kv, kv)
                v_own[2, 16:, at] = kv.T[HEAD_DIM:]
                return 0

            lax.fori_loop(0, N, build_ref, 0, unroll=4)

        f, tile = lax.rem(n // TILES, FRAMES_DEV), lax.rem(n, TILES)
        which = jnp.where(n < phase, f, 2)
        attend(f, tile, k_own.at[which], v_own.at[which])
        return 0

    lax.fori_loop(0, 2 * phase, long_step, 0)

    rest(lambda step: epi_copy(step, other(tm, step), other(tm, step)).wait_recv())
    for f in range(FRAMES_DEV):
        for e in range(ENTRIES):
            kv = r_epi[recv_table[f * ENTRIES + e]]
            used = valid_ref[tm * FRAMES_DEV + f, e] > 0
            stand_in = jnp.where(used, kv, r_kv[f])
            at = slice(e * BLOCK, (e + 1) * BLOCK)
            k_epi[f, at, :] = low_halves(stand_in, stand_in)
            weight = jnp.where(used, 1.0, 0.0).astype(F32)
            v_epi[f, 0:16, at] = jnp.full((16, BLOCK), weight, F32).astype(BF16)
            v_epi[f, 16:, at] = jnp.where(used, kv, jnp.zeros_like(kv)).T[HEAD_DIM:]

    def out_copy(sent, got, to):
        return copy(s_out.at[to], r_out.at[got], sem_out, sent, got, "tok", to)

    per_tile = TILE // BLOCK

    def short_step(n, _):
        f, tile = lax.rem(n, FRAMES_DEV), lax.rem(n // FRAMES_DEV + tok // per_tile, TILES)
        attend(f, tile, k_epi.at[f], v_epi.at[f])

        @pl.when(f == FRAMES_DEV - 1)
        def _():
            both = [acc[g, tile] for g in range(FRAMES_DEV)]
            both = [x[16:] / x[:1] for x in both]
            both = jnp.concatenate(both, axis=0).astype(BF16).T
            s_out[pl.ds(tile * per_tile, per_tile)] = both.reshape(per_tile, BLOCK, 128)
            for b in range(per_tile):
                to = tile * per_tile + b

                @pl.when(to != tok)
                def _():
                    out_copy(to, tok, to).start()

        return 0

    lax.fori_loop(0, phase, short_step, 0)
    r_out[tok] = s_out[tok]
    rest(lambda step: out_copy(other(tok, step), other(tok, step), other(tok, step)).wait_recv())
    for j in range(HEADS // 2):
        lanes = slice(j * 128, (j + 1) * 128)
        a, b = r_out[2 * j], r_out[2 * j + 1]
        o_ref[0, :, lanes] = low_halves(a, b)
        o_ref[1, :, lanes] = high_halves(a, b)

    def drain(step):
        kv_copy(step, tok, other(tok, step)).wait_send()
        q_copy(step, tok, other(tok, step)).wait_send()
        epi_copy(step, tm, other(tm, step)).wait_send()
        out_copy(other(tok, step), tok, other(tok, step)).wait_send()

    rest(drain)
    swap.wait_send()
    hop.wait_send()
    swap_back.wait_send()


def attention(queries, keys, values, epi_dev, epi_frame, epi_block, valid, ref_local):
    vmem, smem = pl.BlockSpec(memory_space=pltpu.VMEM), pl.BlockSpec(memory_space=pltpu.SMEM)
    block = (BLOCK, 128)
    return pl.pallas_call(
        kernel,
        out_shape=jax.ShapeDtypeStruct(queries.shape, BF16),
        in_specs=[vmem] * 3 + [smem] * 5,
        out_specs=vmem,
        scratch_shapes=[
            pltpu.VMEM((2 * N, *block), BF16),
            pltpu.VMEM((N, *block), BF16),
            pltpu.VMEM((2 * N, *block), BF16),
            pltpu.VMEM((N, *block), BF16),
            pltpu.VMEM((2 * N, *block), BF16),
            pltpu.VMEM((2 * N, *block), BF16),
            pltpu.VMEM((2, N, *block), BF16),
            pltpu.VMEM((N // 2, *block), BF16),
            pltpu.VMEM((N, *block), BF16),
            pltpu.VMEM((3, TOKENS, 128), BF16),
            pltpu.VMEM((3, ROWS, TOKENS), BF16),
            pltpu.VMEM((FRAMES_DEV, EPI, 128), BF16),
            pltpu.VMEM((FRAMES_DEV, ROWS, EPI), BF16),
            pltpu.VMEM((FRAMES_DEV, TOKENS, 128), BF16),
            pltpu.VMEM((FRAMES_DEV, TILES, ROWS, TILE), F32),
            pltpu.VMEM((FRAMES_DEV, TILES, 8, TILE), F32),
            pltpu.VMEM((TOKENS, TILE), F32),
            pltpu.VMEM((N, *block), BF16),
            pltpu.VMEM((N, *block), BF16),
            pltpu.SMEM((2 * N,), jnp.int32),
            pltpu.SMEM((FRAMES_DEV * ENTRIES,), jnp.int32),
            pltpu.SemaphoreType.DMA((2, N)),
            pltpu.SemaphoreType.DMA((2, N)),
            pltpu.SemaphoreType.DMA((2, N)),
            pltpu.SemaphoreType.DMA((2, N)),
            pltpu.SemaphoreType.DMA((2, 3)),
        ],
        compiler_params=pltpu.CompilerParams(
            collective_id=0, has_side_effects=True, vmem_limit_bytes=60 * 2**20
        ),
    )(queries, keys, values, epi_dev, epi_frame, epi_block, valid, ref_local)


def solution(mesh):
    shard = P("tm", "tok", None)
    return jax.shard_map(
        attention,
        mesh=mesh,
        in_specs=(shard, shard, shard, P(), P(), P(), P(), P()),
        out_specs=shard,
        check_vma=False,
    )
```

```python
import functools
import math

import jax
import jax.numpy as jnp
from jax import lax
from jax.experimental import pallas as pl
from jax.experimental.pallas import tpu as pltpu
from jax.sharding import PartitionSpec as P

HEADS = 16
HEAD_DIM = 64
BLOCK = 128
FRAMES_DEV = 2
ENTRIES = 6
SPAN = 4
TOKENS = 2048
N = 16
TILE = 1024
CHUNK = 256
TILES = TOKENS // TILE
ROWS = HEAD_DIM + 16
EPI = ENTRIES * BLOCK
QK_SCALE = HEAD_DIM**-0.5 * math.log2(math.e)
MESH = pl.DeviceIdType.MESH
BF16 = jnp.bfloat16
F32 = jnp.float32


def low_halves(a, b):
    return jnp.concatenate([a[:, :HEAD_DIM], b[:, :HEAD_DIM]], axis=1)


def high_halves(a, b):
    return jnp.concatenate([a[:, HEAD_DIM:], b[:, HEAD_DIM:]], axis=1)


def kernel(
    q_ref, k_ref, v_ref, dev_ref, frame_ref, block_ref, valid_ref, local_ref, o_ref,
    s_k, s_v, s_q, s_ref, r_q, r_ref, s_epi_k, s_epi_v, r_epi_k, r_epi_v, s_out, r_out,
    both_k, both_v, cands, cross, r_cross, k_own, v_own, k_epi, v_epi, q_two, acc, top, scores, send_table, recv_table,
    sem_k, sem_v, sem_q, sem_ref, sem_epi_k, sem_epi_v, sem_out, sem_hop,
):
    tm, tok = lax.axis_index("tm"), lax.axis_index("tok")
    core, pair = lax.rem(tm, 2), lax.rem(tm // 2, 2)
    partner, across = tm + 1 - 2 * core, tm + 2 - 4 * pair
    group = tm // SPAN

    def other(me, step):
        return lax.rem(me + step, N)

    def rest(fn):
        lax.fori_loop(1, N, lambda step, _: (fn(step), 0)[1], 0)

    def copy(src, dst, sems, sent, got, axis, to):
        return pltpu.make_async_remote_copy(
            src_ref=src, dst_ref=dst, send_sem=sems.at[0, sent], recv_sem=sems.at[1, got],
            device_id={axis: to}, device_id_type=MESH,
        )

    class Exchange:
        def __init__(self, src, dst, sems, axis):
            self.src, self.dst, self.sems, self.axis = src, dst, sems, axis
            self.me = tm if axis == "tm" else tok

        def to(self, peer):
            return copy(self.src.at[peer], self.dst.at[self.me], self.sems, peer, self.me, self.axis, peer)

        def start(self):
            rest(lambda step: self.to(other(self.me, step)).start())

        def keep(self):
            self.dst[self.me] = self.src[self.me]

        def arrive(self):
            def one(step):
                peer = other(self.me, step)
                copy(self.src.at[peer], self.dst.at[peer], self.sems, peer, peer, self.axis, peer).wait_recv()

            rest(one)

        def drain(self):
            rest(lambda step: self.to(other(self.me, step)).wait_send())

    r_k, r_v = both_k.at[0], both_v.at[0]
    swap_k, swap_v = Exchange(s_k, r_k, sem_k, "tok"), Exchange(s_v, r_v, sem_v, "tok")
    swap_q, swap_ref = Exchange(s_q, r_q, sem_q, "tok"), Exchange(s_ref, r_ref, sem_ref, "tok")
    epi_k, epi_v = Exchange(s_epi_k, r_epi_k, sem_epi_k, "tm"), Exchange(s_epi_v, r_epi_v, sem_epi_v, "tm")
    outs = Exchange(s_out, r_out, sem_out, "tok")

    barrier = pltpu.get_barrier_semaphore()

    def greet(step):
        pl.semaphore_signal(barrier, inc=1, device_id={"tok": other(tok, step)}, device_id_type=MESH)
        pl.semaphore_signal(barrier, inc=1, device_id={"tm": other(tm, step)}, device_id_type=MESH)

    rest(greet)

    def pack(ref, out):
        for j in range(HEADS // 2):
            lanes = slice(j * 128, (j + 1) * 128)
            a, b = ref[0, :, lanes], ref[1, :, lanes]
            out[2 * j] = low_halves(a, b)
            out[2 * j + 1] = high_halves(a, b)

    pack(k_ref, s_k)
    pack(v_ref, s_v)
    pack(q_ref, s_q)
    local = local_ref[group]
    owner_core, owner_pair, ref_bit = lax.rem(local // 2, 2), local // 4, lax.rem(local, 2)
    for j in range(HEADS // 2):
        lanes = slice(j * 128, (j + 1) * 128)
        a, b = k_ref[ref_bit, :, lanes], v_ref[ref_bit, :, lanes]
        cands[core, 2 * j] = low_halves(a, b)
        cands[core, 2 * j + 1] = high_halves(a, b)

    pl.semaphore_wait(barrier, 2 * (N - 1))
    swap = copy(cands.at[core], cands.at[core], sem_hop, 0, 0, "tm", partner)
    swap.start()
    for exchange in (swap_k, swap_v, swap_q):
        exchange.start()
    for exchange in (swap_k, swap_v, swap_q):
        exchange.keep()

    part = N // 2
    mine, theirs = pl.ds(core * part, part), pl.ds((1 - core) * part, part)
    swap.wait_recv()
    cross[...] = cands[owner_core, mine]
    hop = copy(cross, r_cross.at[mine], sem_hop, 1, 1, "tm", across)
    hop.start()

    def fill_send(d, _):
        count, first, second = jnp.int32(0), jnp.int32(0), jnp.int32(0)
        for f in range(FRAMES_DEV):
            for e in range(ENTRIES):
                row = d * FRAMES_DEV + f
                hit = jnp.where(dev_ref[e, row] == tm, 1, 0)
                place = block_ref[e, row] * 2 + frame_ref[e, row]
                first = jnp.where((hit == 1) & (count == 0), place, first)
                second = jnp.where((hit == 1) & (count == 1), place, second)
                count = count + hit
        send_table[d * 2] = first
        send_table[d * 2 + 1] = second
        return 0

    lax.fori_loop(0, N, fill_send, 0)
    names = [dev_ref[e, tm * FRAMES_DEV + f] for f in range(FRAMES_DEV) for e in range(ENTRIES)]
    for i, name in enumerate(names):
        slot = jnp.int32(0)
        for before in names[:i]:
            slot = slot + jnp.where(before == name, 1, 0)
        recv_table[i] = name * 2 + jnp.minimum(slot, 1)

    acc[...] = jnp.zeros_like(acc)
    top[...] = jnp.full_like(top, -1e30)
    for f in range(3):
        v_own[f, 0:16, :] = jnp.ones((16, TOKENS), BF16)

    low = lax.broadcasted_iota(jnp.int32, (BLOCK, 128), 1) < HEAD_DIM

    def over_blocks(fn):
        def one(b, _):
            fn(b, pl.ds(pl.multiple_of(b * BLOCK, BLOCK), BLOCK))
            return 0

        lax.fori_loop(0, N, one, 0, unroll=4)

    def fill_epi(both, s_epi):
        def one(d, _):
            first, second = send_table[d * 2], send_table[d * 2 + 1]
            a, b = both[lax.rem(first, 2), first // 2], both[1 - lax.rem(second, 2), second // 2]
            s_epi[d] = jnp.where(low, a, b)
            return 0

        lax.fori_loop(0, N, one, 0, unroll=4)

    swap_k.arrive()

    def build_k(b, at):
        x = both_k[0, b]
        y = jnp.concatenate([x[:, HEAD_DIM:], x[:, :HEAD_DIM]], axis=1)
        both_k[1, b] = y
        k_own[0, at, :] = jnp.where(low, x, y)
        k_own[1, at, :] = jnp.where(low, y, x)

    over_blocks(build_k)
    fill_epi(both_k, s_epi_k)
    epi_k.start()
    epi_k.keep()

    hop.wait_recv()
    swap_back = copy(r_cross.at[mine], r_cross.at[mine], sem_hop, 2, 2, "tm", partner)
    swap_in = copy(r_cross.at[theirs], r_cross.at[theirs], sem_hop, 2, 2, "tm", partner)
    swap_back.start()

    swap_v.arrive()

    def build_v(b, at):
        x = both_v[0, b]
        both_v[1, b] = jnp.concatenate([x[:, HEAD_DIM:], x[:, :HEAD_DIM]], axis=1)
        x = x.T
        v_own[0, 16:, at] = x[:HEAD_DIM]
        v_own[1, 16:, at] = x[HEAD_DIM:]

    over_blocks(build_v)
    fill_epi(both_v, s_epi_v)
    epi_v.start()
    epi_v.keep()

    swap_in.wait_recv()

    def pick_ref(b, at):
        s_ref[b] = jnp.where(owner_pair == pair, cands[owner_core, b], r_cross[b])

    over_blocks(pick_ref)
    swap_ref.start()
    swap_ref.keep()

    swap_q.arrive()

    def build_q(b, at):
        x = r_q[b].astype(F32) * QK_SCALE
        hi = x.astype(BF16)
        lo = (x - hi.astype(F32)).astype(BF16)
        q_two[0, at, :] = low_halves(hi, lo)
        q_two[1, at, :] = high_halves(hi, lo)

    over_blocks(build_q)

    def attend(f, tile, keys, values):
        rows = pl.ds(pl.multiple_of(tile * TILE, TILE), TILE)
        parts = keys.shape[0] // CHUNK

        def score(c):
            s = lax.dot_general(
                keys[c * CHUNK:(c + 1) * CHUNK, :], q_two[f, rows, :], (((1,), (1,)), ((), ())),
                preferred_element_type=F32,
            )
            scores[c % 2] = s
            return jnp.max(s.reshape(CHUNK // 8, 8, TILE), axis=0)

        peak, old, total = score(0), top[f, tile], acc[f, tile]
        for c in range(parts):
            following = score(c + 1) if c + 1 < parts else None
            new = jnp.maximum(old, jnp.broadcast_to(jnp.max(peak, axis=0, keepdims=True), (8, TILE)))
            probs = jnp.exp2(scores[c % 2] - new[:1]).astype(BF16)
            part_sum = jnp.dot(values[:, c * CHUNK:(c + 1) * CHUNK], probs, preferred_element_type=F32)
            total = total * jnp.exp2(old - new)[:1] + part_sum
            old, peak = new, following
        top[f, tile] = old
        acc[f, tile] = total

    phase = FRAMES_DEV * TILES
    per_tile = TILE // BLOCK

    def build_ref(b, at):
        kv = r_ref[b]
        k_own[2, at, :] = low_halves(kv, kv)
        v_own[2, 16:, at] = kv.T[HEAD_DIM:]

    def half(x, bit):
        return jnp.where(bit == 0, x[:, :HEAD_DIM], x[:, HEAD_DIM:])

    def build_epi():
        for f in range(FRAMES_DEV):
            for e in range(ENTRIES):
                place = recv_table[f * ENTRIES + e]
                source, slot = place // 2, lax.rem(place, 2)
                used = valid_ref[e, tm * FRAMES_DEV + f] > 0
                x, stand_in = half(r_epi_k[source], slot), r_k[0][:, f * HEAD_DIM:(f + 1) * HEAD_DIM]
                x = jnp.where(used, x, stand_in)
                at = slice(e * BLOCK, (e + 1) * BLOCK)
                k_epi[f, at, :] = jnp.concatenate([x, x], axis=1)
                weight = jnp.where(used, 1.0, 0.0).astype(F32)
                v_epi[f, 0:16, at] = jnp.full((16, BLOCK), weight, F32).astype(BF16)
                y = r_epi_v[source]
                y = jnp.where(used, y, jnp.zeros_like(y)).T
                v_epi[f, 16:, at] = jnp.where(slot == 0, y[:HEAD_DIM], y[HEAD_DIM:])

    def long_step(n, _):
        @pl.when(n == phase)
        def _():
            swap_ref.arrive()
            over_blocks(build_ref)

        f, tile = lax.rem(n, FRAMES_DEV), lax.rem(n // FRAMES_DEV, TILES)
        which = jnp.where(n < phase, f, 2)
        attend(f, tile, k_own.at[which], v_own.at[which])
        return 0

    lax.fori_loop(0, 2 * phase, long_step, 0)
    epi_k.arrive()
    epi_v.arrive()
    build_epi()

    def short_step(n, _):
        f, tile = lax.rem(n, FRAMES_DEV), lax.rem(n // FRAMES_DEV + tok // per_tile, TILES)
        attend(f, tile, k_epi.at[f], v_epi.at[f])

        @pl.when(f == FRAMES_DEV - 1)
        def _():
            both = [acc[g, tile] for g in range(FRAMES_DEV)]
            both = [x[16:] / x[:1] for x in both]
            both = jnp.concatenate(both, axis=0).astype(BF16).T
            s_out[pl.ds(tile * per_tile, per_tile)] = both.reshape(per_tile, BLOCK, 128)
            for b in range(per_tile):
                to = tile * per_tile + b

                @pl.when(to != tok)
                def _():
                    outs.to(to).start()

        return 0

    lax.fori_loop(0, phase, short_step, 0)
    outs.keep()
    for exchange in (swap_k, swap_v, swap_q, swap_ref, epi_k, epi_v):
        exchange.drain()
    swap.wait_send()
    hop.wait_send()
    swap_back.wait_send()
    outs.arrive()
    for j in range(HEADS // 2):
        lanes = slice(j * 128, (j + 1) * 128)
        a, b = r_out[2 * j], r_out[2 * j + 1]
        o_ref[0, :, lanes] = low_halves(a, b)
        o_ref[1, :, lanes] = high_halves(a, b)
    outs.drain()


def attention(queries, keys, values, epi_dev, epi_frame, epi_block, valid, ref_local):
    vmem, smem = pl.BlockSpec(memory_space=pltpu.VMEM), pl.BlockSpec(memory_space=pltpu.SMEM)
    blocks = pltpu.VMEM((N, BLOCK, 128), BF16)
    tables = [x.T for x in (epi_dev, epi_frame, epi_block, valid)]
    return pl.pallas_call(
        kernel,
        out_shape=jax.ShapeDtypeStruct(queries.shape, BF16),
        in_specs=[vmem] * 3 + [smem] * 5,
        out_specs=vmem,
        scratch_shapes=[
            *[blocks] * 12,
            *[pltpu.VMEM((2, N, BLOCK, 128), BF16)] * 2,
            pltpu.VMEM((2, N, BLOCK, 128), BF16),
            pltpu.VMEM((N // 2, BLOCK, 128), BF16),
            blocks,
            pltpu.VMEM((3, TOKENS, 128), BF16),
            pltpu.VMEM((3, ROWS, TOKENS), BF16),
            pltpu.VMEM((FRAMES_DEV, EPI, 128), BF16),
            pltpu.VMEM((FRAMES_DEV, ROWS, EPI), BF16),
            pltpu.VMEM((FRAMES_DEV, TOKENS, 128), BF16),
            pltpu.VMEM((FRAMES_DEV, TILES, ROWS, TILE), F32),
            pltpu.VMEM((FRAMES_DEV, TILES, 8, TILE), F32),
            pltpu.VMEM((2, CHUNK, TILE), F32),
            pltpu.SMEM((2 * N,), jnp.int32),
            pltpu.SMEM((FRAMES_DEV * ENTRIES,), jnp.int32),
            *[pltpu.SemaphoreType.DMA((2, N))] * 7,
            pltpu.SemaphoreType.DMA((2, 3)),
        ],
        compiler_params=pltpu.CompilerParams(
            collective_id=0, has_side_effects=True, vmem_limit_bytes=60 * 2**20
        ),
    )(queries, keys, values, *tables, ref_local)


def solution(mesh):
    shard = P("tm", "tok", None)
    return jax.shard_map(
        attention,
        mesh=mesh,
        in_specs=(shard, shard, shard, P(), P(), P(), P(), P()),
        out_specs=shard,
        check_vma=False,
    )
```

```python
import functools
import math

import jax
import jax.numpy as jnp
from jax import lax
from jax.experimental import pallas as pl
from jax.experimental.pallas import tpu as pltpu
from jax.sharding import PartitionSpec as P

HEADS = 16
HEAD_DIM = 64
BLOCK = 128
FRAMES_DEV = 2
ENTRIES = 6
SPAN = 4
TOKENS = 2048
N = 16
TILE = 1024
CHUNK = 256
COLUMN = 256
DEPTH = 8
TILES = TOKENS // TILE
ROWS = HEAD_DIM + 16
EPI = ENTRIES * BLOCK
QK_SCALE = HEAD_DIM**-0.5 * math.log2(math.e)
MESH = pl.DeviceIdType.MESH
BF16 = jnp.bfloat16
F32 = jnp.float32


def low_halves(a, b):
    return jnp.concatenate([a[:, :HEAD_DIM], b[:, :HEAD_DIM]], axis=1)


def high_halves(a, b):
    return jnp.concatenate([a[:, HEAD_DIM:], b[:, HEAD_DIM:]], axis=1)


def kernel(
    q_ref, k_ref, v_ref, dev_ref, frame_ref, block_ref, valid_ref, local_ref, o_ref,
    s_k, s_v, s_q, s_ref, r_q, r_ref, s_epi_k, s_epi_v, r_epi_k, r_epi_v, s_out, r_out,
    both_k, both_v, cands, cross, r_cross, k_own, v_own, k_epi, v_epi, q_two, acc, top, scores, send_table, recv_table,
    sem_k, sem_v, sem_q, sem_ref, sem_epi_k, sem_epi_v, sem_out, sem_hop,
):
    tm, tok = lax.axis_index("tm"), lax.axis_index("tok")
    core, pair = lax.rem(tm, 2), lax.rem(tm // 2, 2)
    partner, across = tm + 1 - 2 * core, tm + 2 - 4 * pair
    group = tm // SPAN

    def other(me, step):
        return lax.rem(me + step, N)

    def rest(fn):
        lax.fori_loop(1, N, lambda step, _: (fn(step), 0)[1], 0)

    def copy(src, dst, sems, sent, got, axis, to):
        return pltpu.make_async_remote_copy(
            src_ref=src, dst_ref=dst, send_sem=sems.at[0, sent], recv_sem=sems.at[1, got],
            device_id={axis: to}, device_id_type=MESH,
        )

    class Exchange:
        def __init__(self, src, dst, sems, axis):
            self.src, self.dst, self.sems, self.axis = src, dst, sems, axis
            self.me = tm if axis == "tm" else tok

        def to(self, peer):
            return copy(self.src.at[peer], self.dst.at[self.me], self.sems, peer, self.me, self.axis, peer)

        def start(self):
            rest(lambda step: self.to(other(self.me, step)).start())

        def keep(self):
            self.dst[self.me] = self.src[self.me]

        def arrive(self):
            def one(step):
                peer = other(self.me, step)
                copy(self.src.at[peer], self.dst.at[peer], self.sems, peer, peer, self.axis, peer).wait_recv()

            rest(one)

        def drain(self):
            rest(lambda step: self.to(other(self.me, step)).wait_send())

    r_k, r_v = both_k.at[0], both_v.at[0]
    swap_k, swap_v = Exchange(s_k, r_k, sem_k, "tok"), Exchange(s_v, r_v, sem_v, "tok")
    swap_q, swap_ref = Exchange(s_q, r_q, sem_q, "tok"), Exchange(s_ref, r_ref, sem_ref, "tok")
    epi_k, epi_v = Exchange(s_epi_k, r_epi_k, sem_epi_k, "tm"), Exchange(s_epi_v, r_epi_v, sem_epi_v, "tm")
    outs = Exchange(s_out, r_out, sem_out, "tok")

    barrier = pltpu.get_barrier_semaphore()

    def greet(step):
        pl.semaphore_signal(barrier, inc=1, device_id={"tok": other(tok, step)}, device_id_type=MESH)
        pl.semaphore_signal(barrier, inc=1, device_id={"tm": other(tm, step)}, device_id_type=MESH)

    rest(greet)

    def pack(ref, out):
        for j in range(HEADS // 2):
            lanes = slice(j * 128, (j + 1) * 128)
            a, b = ref[0, :, lanes], ref[1, :, lanes]
            out[2 * j] = low_halves(a, b)
            out[2 * j + 1] = high_halves(a, b)

    pack(k_ref, s_k)
    pack(v_ref, s_v)
    pack(q_ref, s_q)
    local = local_ref[group]
    owner_core, owner_pair, ref_bit = lax.rem(local // 2, 2), local // 4, lax.rem(local, 2)
    for j in range(HEADS // 2):
        lanes = slice(j * 128, (j + 1) * 128)
        a, b = k_ref[ref_bit, :, lanes], v_ref[ref_bit, :, lanes]
        cands[core, 2 * j] = low_halves(a, b)
        cands[core, 2 * j + 1] = high_halves(a, b)

    pl.semaphore_wait(barrier, 2 * (N - 1))
    swap = copy(cands.at[core], cands.at[core], sem_hop, 0, 0, "tm", partner)
    swap.start()
    for exchange in (swap_k, swap_v, swap_q):
        exchange.start()
    for exchange in (swap_k, swap_v, swap_q):
        exchange.keep()

    part = N // 2
    mine, theirs = pl.ds(core * part, part), pl.ds((1 - core) * part, part)
    swap.wait_recv()
    cross[...] = cands[owner_core, mine]
    hop = copy(cross, r_cross.at[mine], sem_hop, 1, 1, "tm", across)
    hop.start()

    def fill_send(d, _):
        count, first, second = jnp.int32(0), jnp.int32(0), jnp.int32(0)
        for f in range(FRAMES_DEV):
            for e in range(ENTRIES):
                row = d * FRAMES_DEV + f
                hit = jnp.where(dev_ref[e, row] == tm, 1, 0)
                place = block_ref[e, row] * 2 + frame_ref[e, row]
                first = jnp.where((hit == 1) & (count == 0), place, first)
                second = jnp.where((hit == 1) & (count == 1), place, second)
                count = count + hit
        send_table[d * 2] = first
        send_table[d * 2 + 1] = second
        return 0

    lax.fori_loop(0, N, fill_send, 0)
    names = [dev_ref[e, tm * FRAMES_DEV + f] for f in range(FRAMES_DEV) for e in range(ENTRIES)]
    for i, name in enumerate(names):
        slot = jnp.int32(0)
        for before in names[:i]:
            slot = slot + jnp.where(before == name, 1, 0)
        recv_table[i] = name * 2 + jnp.minimum(slot, 1)

    acc[...] = jnp.zeros_like(acc)
    top[...] = jnp.full_like(top, -1e30)
    for f in range(3):
        v_own[f, 0:16, :] = jnp.ones((16, TOKENS), BF16)

    low = lax.broadcasted_iota(jnp.int32, (BLOCK, 128), 1) < HEAD_DIM

    def over_blocks(fn):
        def one(b, _):
            fn(b, pl.ds(pl.multiple_of(b * BLOCK, BLOCK), BLOCK))
            return 0

        lax.fori_loop(0, N, one, 0, unroll=4)

    def fill_epi(both, s_epi):
        def one(d, _):
            first, second = send_table[d * 2], send_table[d * 2 + 1]
            a, b = both[lax.rem(first, 2), first // 2], both[1 - lax.rem(second, 2), second // 2]
            s_epi[d] = jnp.where(low, a, b)
            return 0

        lax.fori_loop(0, N, one, 0, unroll=4)

    swap_k.arrive()

    def build_k(b, at):
        x = both_k[0, b]
        y = jnp.concatenate([x[:, HEAD_DIM:], x[:, :HEAD_DIM]], axis=1)
        both_k[1, b] = y
        k_own[0, at, :] = jnp.where(low, x, y)
        k_own[1, at, :] = jnp.where(low, y, x)

    over_blocks(build_k)
    fill_epi(both_k, s_epi_k)
    epi_k.start()
    epi_k.keep()

    hop.wait_recv()
    swap_back = copy(r_cross.at[mine], r_cross.at[mine], sem_hop, 2, 2, "tm", partner)
    swap_in = copy(r_cross.at[theirs], r_cross.at[theirs], sem_hop, 2, 2, "tm", partner)
    swap_back.start()

    swap_v.arrive()

    def build_v(b, at):
        x = both_v[0, b]
        both_v[1, b] = jnp.concatenate([x[:, HEAD_DIM:], x[:, :HEAD_DIM]], axis=1)
        x = x.T
        v_own[0, 16:, at] = x[:HEAD_DIM]
        v_own[1, 16:, at] = x[HEAD_DIM:]

    over_blocks(build_v)
    fill_epi(both_v, s_epi_v)
    epi_v.start()
    epi_v.keep()

    swap_in.wait_recv()

    def pick_ref(b, at):
        s_ref[b] = jnp.where(owner_pair == pair, cands[owner_core, b], r_cross[b])

    over_blocks(pick_ref)
    swap_ref.start()
    swap_ref.keep()

    swap_q.arrive()

    def build_q(b, at):
        x = r_q[b].astype(F32) * QK_SCALE
        hi = x.astype(BF16)
        lo = (x - hi.astype(F32)).astype(BF16)
        q_two[0, at, :] = low_halves(hi, lo)
        q_two[1, at, :] = high_halves(hi, lo)

    over_blocks(build_q)

    def attend(work, keys, values):
        def score(i):
            f, column, c = work[i]
            rows = pl.ds(pl.multiple_of(column * COLUMN, COLUMN), COLUMN)
            s = lax.dot_general(
                keys(f)[c * CHUNK:(c + 1) * CHUNK, :], q_two[f, rows, :], (((1,), (1,)), ((), ())),
                preferred_element_type=F32,
            )
            scores[i % (DEPTH + 1)] = s
            return jnp.max(s.reshape(CHUNK // 8, 8, COLUMN), axis=0)

        peaks = {i: score(i) for i in range(DEPTH)}
        for i, (f, column, c) in enumerate(work):
            if i + DEPTH < len(work):
                peaks[i + DEPTH] = score(i + DEPTH)
            old = top[f, column]
            peak = jnp.max(peaks.pop(i), axis=0, keepdims=True)
            new = jnp.maximum(old, jnp.broadcast_to(peak, (8, COLUMN)))
            probs = jnp.exp2(scores[i % (DEPTH + 1)] - new[:1]).astype(BF16)
            part_sum = jnp.dot(values(f)[:, c * CHUNK:(c + 1) * CHUNK], probs, preferred_element_type=F32)
            acc[f, column] = acc[f, column] * jnp.exp2(old - new)[:1] + part_sum
            top[f, column] = new

    per_tile, columns = TILE // BLOCK, TILE // COLUMN

    def build_ref(b, at):
        kv = r_ref[b]
        k_own[2, at, :] = low_halves(kv, kv)
        v_own[2, 16:, at] = kv.T[HEAD_DIM:]

    def half(x, bit):
        return jnp.where(bit == 0, x[:, :HEAD_DIM], x[:, HEAD_DIM:])

    def build_epi():
        for f in range(FRAMES_DEV):
            for e in range(ENTRIES):
                place = recv_table[f * ENTRIES + e]
                source, slot = place // 2, lax.rem(place, 2)
                used = valid_ref[e, tm * FRAMES_DEV + f] > 0
                x, stand_in = half(r_epi_k[source], slot), r_k[0][:, f * HEAD_DIM:(f + 1) * HEAD_DIM]
                x = jnp.where(used, x, stand_in)
                at = slice(e * BLOCK, (e + 1) * BLOCK)
                k_epi[f, at, :] = jnp.concatenate([x, x], axis=1)
                weight = jnp.where(used, 1.0, 0.0).astype(F32)
                v_epi[f, 0:16, at] = jnp.full((16, BLOCK), weight, F32).astype(BF16)
                y = r_epi_v[source]
                y = jnp.where(used, y, jnp.zeros_like(y)).T
                v_epi[f, 16:, at] = jnp.where(slot == 0, y[:HEAD_DIM], y[HEAD_DIM:])

    def long_step(n, _):
        @pl.when(n == FRAMES_DEV)
        def _():
            swap_ref.arrive()
            over_blocks(build_ref)

        which = jnp.where(n < FRAMES_DEV, n, 2)
        work = [(lax.rem(n, FRAMES_DEV), t, c) for c in range(TOKENS // CHUNK) for t in range(TOKENS // COLUMN)]
        attend(work, lambda f: k_own.at[which], lambda f: v_own.at[which])
        return 0

    lax.fori_loop(0, 2 * FRAMES_DEV, long_step, 0)
    epi_k.arrive()
    epi_v.arrive()
    build_epi()

    def short_step(n, _):
        tile = lax.rem(n + tok // per_tile, TILES)
        work = [
            (f, tile * columns + t, c)
            for f in range(FRAMES_DEV) for c in range(EPI // CHUNK) for t in range(columns)
        ]
        attend(work, lambda f: k_epi.at[f], lambda f: v_epi.at[f])
        for t in range(columns):
            both = [acc[f, tile * columns + t] for f in range(FRAMES_DEV)]
            both = jnp.concatenate([x[16:] / x[:1] for x in both], axis=0).astype(BF16).T
            s_out[pl.ds(tile * per_tile + t * (COLUMN // BLOCK), COLUMN // BLOCK)] = both.reshape(-1, BLOCK, 128)
        for b in range(per_tile):
            to = tile * per_tile + b

            @pl.when(to != tok)
            def _():
                outs.to(to).start()

        return 0

    lax.fori_loop(0, TILES, short_step, 0)
    outs.keep()
    for exchange in (swap_k, swap_v, swap_q, swap_ref, epi_k, epi_v):
        exchange.drain()
    swap.wait_send()
    hop.wait_send()
    swap_back.wait_send()
    outs.arrive()
    for j in range(HEADS // 2):
        lanes = slice(j * 128, (j + 1) * 128)
        a, b = r_out[2 * j], r_out[2 * j + 1]
        o_ref[0, :, lanes] = low_halves(a, b)
        o_ref[1, :, lanes] = high_halves(a, b)
    outs.drain()


def attention(queries, keys, values, epi_dev, epi_frame, epi_block, valid, ref_local):
    vmem, smem = pl.BlockSpec(memory_space=pltpu.VMEM), pl.BlockSpec(memory_space=pltpu.SMEM)
    blocks = pltpu.VMEM((N, BLOCK, 128), BF16)
    tables = [x.T for x in (epi_dev, epi_frame, epi_block, valid)]
    return pl.pallas_call(
        kernel,
        out_shape=jax.ShapeDtypeStruct(queries.shape, BF16),
        in_specs=[vmem] * 3 + [smem] * 5,
        out_specs=vmem,
        scratch_shapes=[
            *[blocks] * 12,
            *[pltpu.VMEM((2, N, BLOCK, 128), BF16)] * 2,
            pltpu.VMEM((2, N, BLOCK, 128), BF16),
            pltpu.VMEM((N // 2, BLOCK, 128), BF16),
            blocks,
            pltpu.VMEM((3, TOKENS, 128), BF16),
            pltpu.VMEM((3, ROWS, TOKENS), BF16),
            pltpu.VMEM((FRAMES_DEV, EPI, 128), BF16),
            pltpu.VMEM((FRAMES_DEV, ROWS, EPI), BF16),
            pltpu.VMEM((FRAMES_DEV, TOKENS, 128), BF16),
            pltpu.VMEM((FRAMES_DEV, TOKENS // COLUMN, ROWS, COLUMN), F32),
            pltpu.VMEM((FRAMES_DEV, TOKENS // COLUMN, 8, COLUMN), F32),
            pltpu.VMEM((DEPTH + 1, CHUNK, COLUMN), F32),
            pltpu.SMEM((2 * N,), jnp.int32),
            pltpu.SMEM((FRAMES_DEV * ENTRIES,), jnp.int32),
            *[pltpu.SemaphoreType.DMA((2, N))] * 7,
            pltpu.SemaphoreType.DMA((2, 3)),
        ],
        compiler_params=pltpu.CompilerParams(
            collective_id=0, has_side_effects=True, vmem_limit_bytes=60 * 2**20
        ),
    )(queries, keys, values, *tables, ref_local)


def solution(mesh):
    shard = P("tm", "tok", None)
    return jax.shard_map(
        attention,
        mesh=mesh,
        in_specs=(shard, shard, shard, P(), P(), P(), P(), P()),
        out_specs=shard,
        check_vma=False,
    )
```

```python
import functools
import math

import jax
import jax.numpy as jnp
from jax import lax
from jax.experimental import pallas as pl
from jax.experimental.pallas import tpu as pltpu
from jax.sharding import PartitionSpec as P

HEADS = 16
HEAD_DIM = 64
BLOCK = 128
FRAMES_DEV = 2
ENTRIES = 6
SPAN = 4
TOKENS = 2048
N = 16
TILE = 1024
CHUNK = 256
COLUMN = 256
DEPTH = 8
TILES = TOKENS // TILE
ROWS = HEAD_DIM + 16
EPI = ENTRIES * BLOCK
QK_SCALE = HEAD_DIM**-0.5 * math.log2(math.e)
MESH = pl.DeviceIdType.MESH
BF16 = jnp.bfloat16
F32 = jnp.float32


def low_halves(a, b):
    return jnp.concatenate([a[:, :HEAD_DIM], b[:, :HEAD_DIM]], axis=1)


def high_halves(a, b):
    return jnp.concatenate([a[:, HEAD_DIM:], b[:, HEAD_DIM:]], axis=1)


def kernel(
    q_hbm, k_hbm, v_hbm, dev_ref, frame_ref, block_ref, valid_ref, local_ref, o_ref,
    q_ref, k_ref, v_ref, s_k, s_v, s_q, s_ref, r_q, r_ref, s_epi_k, s_epi_v, r_epi_k, r_epi_v, s_out, r_out,
    both_k, both_v, cands, cross, r_cross, k_own, v_own, k_epi, v_epi, q_two, acc, top, scores, send_table,
    sem_k, sem_v, sem_q, sem_ref, sem_epi_k, sem_epi_v, sem_out, sem_hop, sem_in,
):
    tm, tok = lax.axis_index("tm"), lax.axis_index("tok")
    core, pair = lax.rem(tm, 2), lax.rem(tm // 2, 2)
    partner, across = tm + 1 - 2 * core, tm + 2 - 4 * pair
    group = tm // SPAN

    def other(me, step):
        return lax.rem(me + step, N)

    def rest(fn):
        lax.fori_loop(1, N, lambda step, _: (fn(step), 0)[1], 0)

    def copy(src, dst, sems, sent, got, axis, to):
        return pltpu.make_async_remote_copy(
            src_ref=src, dst_ref=dst, send_sem=sems.at[0, sent], recv_sem=sems.at[1, got],
            device_id={axis: to}, device_id_type=MESH,
        )

    class Exchange:
        def __init__(self, src, dst, sems, axis):
            self.src, self.dst, self.sems, self.axis = src, dst, sems, axis
            self.me = tm if axis == "tm" else tok

        def to(self, peer):
            return copy(self.src.at[peer], self.dst.at[self.me], self.sems, peer, self.me, self.axis, peer)

        def start(self):
            rest(lambda step: self.to(other(self.me, step)).start())

        def keep(self):
            self.dst[self.me] = self.src[self.me]

        def arrive(self):
            def one(step):
                peer = other(self.me, step)
                copy(self.src.at[peer], self.dst.at[peer], self.sems, peer, peer, self.axis, peer).wait_recv()

            rest(one)

        def drain(self):
            rest(lambda step: self.to(other(self.me, step)).wait_send())

    r_k, r_v = both_k.at[0], both_v.at[0]
    swap_k, swap_v = Exchange(s_k, r_k, sem_k, "tok"), Exchange(s_v, r_v, sem_v, "tok")
    swap_q, swap_ref = Exchange(s_q, r_q, sem_q, "tok"), Exchange(s_ref, r_ref, sem_ref, "tok")
    epi_k, epi_v = Exchange(s_epi_k, r_epi_k, sem_epi_k, "tm"), Exchange(s_epi_v, r_epi_v, sem_epi_v, "tm")
    outs = Exchange(s_out, r_out, sem_out, "tok")

    barrier = pltpu.get_barrier_semaphore()

    def greet(step):
        pl.semaphore_signal(barrier, inc=1, device_id={"tok": other(tok, step)}, device_id_type=MESH)
        pl.semaphore_signal(barrier, inc=1, device_id={"tm": other(tm, step)}, device_id_type=MESH)

    fetches = [
        pltpu.make_async_copy(src, dst, sem_in.at[i])
        for i, (src, dst) in enumerate(((k_hbm, k_ref), (v_hbm, v_ref), (q_hbm, q_ref)))
    ]
    for fetch in fetches:
        fetch.start()
    rest(greet)

    def pack(ref, out):
        for j in range(HEADS // 2):
            lanes = slice(j * 128, (j + 1) * 128)
            a, b = ref[0, :, lanes], ref[1, :, lanes]
            out[2 * j] = low_halves(a, b)
            out[2 * j + 1] = high_halves(a, b)

    for fetch, ref, out in zip(fetches, (k_ref, v_ref, q_ref), (s_k, s_v, s_q)):
        fetch.wait()
        pack(ref, out)
    local = local_ref[group]
    owner_core, owner_pair, ref_bit = lax.rem(local // 2, 2), local // 4, lax.rem(local, 2)
    for j in range(HEADS // 2):
        lanes = slice(j * 128, (j + 1) * 128)
        a, b = k_ref[ref_bit, :, lanes], v_ref[ref_bit, :, lanes]
        cands[core, 2 * j] = low_halves(a, b)
        cands[core, 2 * j + 1] = high_halves(a, b)

    pl.semaphore_wait(barrier, 2 * (N - 1))
    swap = copy(cands.at[core], cands.at[core], sem_hop, 0, 0, "tm", partner)
    swap.start()
    for exchange in (swap_k, swap_v, swap_q):
        exchange.start()
    for exchange in (swap_k, swap_v, swap_q):
        exchange.keep()

    part = N // 2
    mine, theirs = pl.ds(core * part, part), pl.ds((1 - core) * part, part)
    swap.wait_recv()
    cross[...] = cands[owner_core, mine]
    hop = copy(cross, r_cross.at[mine], sem_hop, 1, 1, "tm", across)
    hop.start()

    def fill_send(d, _):
        for f in range(FRAMES_DEV):
            row, place = d * FRAMES_DEV + f, jnp.int32(0)
            for e in range(ENTRIES):
                spot = block_ref[e, row] * 2 + frame_ref[e, row]
                place = jnp.where(dev_ref[e, row] == tm, spot, place)
            send_table[d * 2 + f] = place
        return 0

    lax.fori_loop(0, N, fill_send, 0)

    acc[...] = jnp.zeros_like(acc)
    top[...] = jnp.full_like(top, -1e30)
    for f in range(3):
        v_own[f, 0:16, :] = jnp.ones((16, TOKENS), BF16)

    low = lax.broadcasted_iota(jnp.int32, (BLOCK, 128), 1) < HEAD_DIM

    def over_blocks(fn):
        def one(b, _):
            fn(b, pl.ds(pl.multiple_of(b * BLOCK, BLOCK), BLOCK))
            return 0

        lax.fori_loop(0, N, one, 0, unroll=4)

    def fill_epi(both, s_epi):
        def one(d, _):
            first, second = send_table[d * 2], send_table[d * 2 + 1]
            a, b = both[lax.rem(first, 2), first // 2], both[1 - lax.rem(second, 2), second // 2]
            s_epi[d] = jnp.where(low, a, b)
            return 0

        lax.fori_loop(0, N, one, 0, unroll=4)

    swap_k.arrive()

    def build_k(b, at):
        x = both_k[0, b]
        y = jnp.concatenate([x[:, HEAD_DIM:], x[:, :HEAD_DIM]], axis=1)
        both_k[1, b] = y
        k_own[0, at, :] = jnp.where(low, x, y)
        k_own[1, at, :] = jnp.where(low, y, x)

    over_blocks(build_k)
    fill_epi(both_k, s_epi_k)
    epi_k.start()
    epi_k.keep()

    hop.wait_recv()
    swap_back = copy(r_cross.at[mine], r_cross.at[mine], sem_hop, 2, 2, "tm", partner)
    swap_in = copy(r_cross.at[theirs], r_cross.at[theirs], sem_hop, 2, 2, "tm", partner)
    swap_back.start()

    swap_v.arrive()

    def build_v(b, at):
        x = both_v[0, b]
        both_v[1, b] = jnp.concatenate([x[:, HEAD_DIM:], x[:, :HEAD_DIM]], axis=1)
        x = x.T
        v_own[0, 16:, at] = x[:HEAD_DIM]
        v_own[1, 16:, at] = x[HEAD_DIM:]

    over_blocks(build_v)
    fill_epi(both_v, s_epi_v)
    epi_v.start()
    epi_v.keep()

    swap_in.wait_recv()

    def pick_ref(b, at):
        s_ref[b] = jnp.where(owner_pair == pair, cands[owner_core, b], r_cross[b])

    over_blocks(pick_ref)
    swap_ref.start()
    swap_ref.keep()

    swap_q.arrive()

    def build_q(b, at):
        x = r_q[b].astype(F32) * QK_SCALE
        hi = x.astype(BF16)
        lo = (x - hi.astype(F32)).astype(BF16)
        q_two[0, at, :] = low_halves(hi, lo)
        q_two[1, at, :] = high_halves(hi, lo)

    over_blocks(build_q)

    def attend(work, keys, values):
        def score(i):
            f, column, c = work[i]
            rows = pl.ds(pl.multiple_of(column * COLUMN, COLUMN), COLUMN)
            s = lax.dot_general(
                keys(f)[c * CHUNK:(c + 1) * CHUNK, :], q_two[f, rows, :], (((1,), (1,)), ((), ())),
                preferred_element_type=F32,
            )
            scores[i % (DEPTH + 1)] = s
            return jnp.max(s.reshape(CHUNK // 8, 8, COLUMN), axis=0)

        peaks = {i: score(i) for i in range(DEPTH)}
        for i, (f, column, c) in enumerate(work):
            if i + DEPTH < len(work):
                peaks[i + DEPTH] = score(i + DEPTH)
            old = top[f, column]
            peak = jnp.max(peaks.pop(i), axis=0, keepdims=True)
            new = jnp.maximum(old, jnp.broadcast_to(peak, (8, COLUMN)))
            probs = jnp.exp2(scores[i % (DEPTH + 1)] - new[:1]).astype(BF16)
            part_sum = jnp.dot(values(f)[:, c * CHUNK:(c + 1) * CHUNK], probs, preferred_element_type=F32)
            acc[f, column] = acc[f, column] * jnp.exp2(old - new)[:1] + part_sum
            top[f, column] = new

    per_tile, columns = TILE // BLOCK, TILE // COLUMN

    def build_ref(b, at):
        kv = r_ref[b]
        k_own[2, at, :] = low_halves(kv, kv)
        v_own[2, 16:, at] = kv.T[HEAD_DIM:]

    def build_epi():
        for f in range(FRAMES_DEV):
            side = slice(f * HEAD_DIM, (f + 1) * HEAD_DIM)
            for e in range(ENTRIES):
                row, at = tm * FRAMES_DEV + f, slice(e * BLOCK, (e + 1) * BLOCK)
                source, used = dev_ref[e, row], valid_ref[e, row] > 0
                x = jnp.where(used, r_epi_k[source][:, side], r_k[0][:, side])
                k_epi[f, at, :] = jnp.concatenate([x, x], axis=1)
                weight = jnp.where(used, 1.0, 0.0).astype(F32)
                v_epi[f, 0:16, at] = jnp.full((16, BLOCK), weight, F32).astype(BF16)
                y = r_epi_v[source]
                v_epi[f, 16:, at] = jnp.where(used, y, jnp.zeros_like(y)).T[side]

    def long_step(n, _):
        @pl.when(n == FRAMES_DEV)
        def _():
            swap_ref.arrive()
            over_blocks(build_ref)

        which = jnp.where(n < FRAMES_DEV, n, 2)
        work = [(lax.rem(n, FRAMES_DEV), t, c) for c in range(TOKENS // CHUNK) for t in range(TOKENS // COLUMN)]
        attend(work, lambda f: k_own.at[which], lambda f: v_own.at[which])
        return 0

    lax.fori_loop(0, 2 * FRAMES_DEV, long_step, 0)
    epi_k.arrive()
    epi_v.arrive()
    build_epi()

    def short_step(n, _):
        tile = lax.rem(n + tok // per_tile, TILES)
        work = [
            (f, tile * columns + t, c)
            for f in range(FRAMES_DEV) for c in range(EPI // CHUNK) for t in range(columns)
        ]
        attend(work, lambda f: k_epi.at[f], lambda f: v_epi.at[f])
        for t in range(columns):
            both = [acc[f, tile * columns + t] for f in range(FRAMES_DEV)]
            both = jnp.concatenate([x[16:] / x[:1] for x in both], axis=0).astype(BF16).T
            s_out[pl.ds(tile * per_tile + t * (COLUMN // BLOCK), COLUMN // BLOCK)] = both.reshape(-1, BLOCK, 128)
        for b in range(per_tile):
            to = tile * per_tile + b

            @pl.when(to != tok)
            def _():
                outs.to(to).start()

        return 0

    lax.fori_loop(0, TILES, short_step, 0)
    outs.keep()
    for exchange in (swap_k, swap_v, swap_q, swap_ref, epi_k, epi_v):
        exchange.drain()
    swap.wait_send()
    hop.wait_send()
    swap_back.wait_send()
    outs.arrive()
    for j in range(HEADS // 2):
        lanes = slice(j * 128, (j + 1) * 128)
        a, b = r_out[2 * j], r_out[2 * j + 1]
        o_ref[0, :, lanes] = low_halves(a, b)
        o_ref[1, :, lanes] = high_halves(a, b)
    outs.drain()


def attention(queries, keys, values, epi_dev, epi_frame, epi_block, valid, ref_local):
    vmem, smem = pl.BlockSpec(memory_space=pltpu.VMEM), pl.BlockSpec(memory_space=pltpu.SMEM)
    blocks = pltpu.VMEM((N, BLOCK, 128), BF16)
    tables = [x.T for x in (epi_dev, epi_frame, epi_block, valid)]
    return pl.pallas_call(
        kernel,
        out_shape=jax.ShapeDtypeStruct(queries.shape, BF16),
        in_specs=[pl.BlockSpec(memory_space=pl.ANY)] * 3 + [smem] * 5,
        out_specs=vmem,
        scratch_shapes=[
            *[pltpu.VMEM(queries.shape, BF16)] * 3,
            *[blocks] * 12,
            *[pltpu.VMEM((2, N, BLOCK, 128), BF16)] * 2,
            pltpu.VMEM((2, N, BLOCK, 128), BF16),
            pltpu.VMEM((N // 2, BLOCK, 128), BF16),
            blocks,
            pltpu.VMEM((3, TOKENS, 128), BF16),
            pltpu.VMEM((3, ROWS, TOKENS), BF16),
            pltpu.VMEM((FRAMES_DEV, EPI, 128), BF16),
            pltpu.VMEM((FRAMES_DEV, ROWS, EPI), BF16),
            pltpu.VMEM((FRAMES_DEV, TOKENS, 128), BF16),
            pltpu.VMEM((FRAMES_DEV, TOKENS // COLUMN, ROWS, COLUMN), F32),
            pltpu.VMEM((FRAMES_DEV, TOKENS // COLUMN, 8, COLUMN), F32),
            pltpu.VMEM((DEPTH + 1, CHUNK, COLUMN), F32),
            pltpu.SMEM((2 * N,), jnp.int32),
            *[pltpu.SemaphoreType.DMA((2, N))] * 7,
            pltpu.SemaphoreType.DMA((2, 3)),
            pltpu.SemaphoreType.DMA((3,)),
        ],
        compiler_params=pltpu.CompilerParams(
            collective_id=0, has_side_effects=True, vmem_limit_bytes=60 * 2**20
        ),
    )(queries, keys, values, *tables, ref_local)


def solution(mesh):
    shard = P("tm", "tok", None)
    return jax.shard_map(
        attention,
        mesh=mesh,
        in_specs=(shard, shard, shard, P(), P(), P(), P(), P()),
        out_specs=shard,
        check_vma=False,
    )
```

```python
import functools
import math

import jax
import jax.numpy as jnp
from jax import lax
from jax.experimental import pallas as pl
from jax.experimental.pallas import tpu as pltpu
from jax.sharding import PartitionSpec as P

HEADS = 16
HEAD_DIM = 64
BLOCK = 128
FRAMES_DEV = 2
ENTRIES = 6
SPAN = 4
TOKENS = 2048
N = 16
TILE = 1024
CHUNK = 256
COLUMN = 256
DEPTH = 8
TILES = TOKENS // TILE
ROWS = HEAD_DIM + 16
EPI = ENTRIES * BLOCK
QK_SCALE = HEAD_DIM**-0.5 * math.log2(math.e)
MESH = pl.DeviceIdType.MESH
SIDE = 4
FAR_FIRST = sorted(
    ((dx, dy) for dx in range(SIDE) for dy in range(SIDE) if dx or dy),
    key=lambda d: -(min(d[0], SIDE - d[0]) + min(d[1], SIDE - d[1])),
)
BF16 = jnp.bfloat16
F32 = jnp.float32


def low_halves(a, b):
    return jnp.concatenate([a[:, :HEAD_DIM], b[:, :HEAD_DIM]], axis=1)


def high_halves(a, b):
    return jnp.concatenate([a[:, HEAD_DIM:], b[:, HEAD_DIM:]], axis=1)


def kernel(
    q_hbm, k_hbm, v_hbm, dev_ref, frame_ref, block_ref, valid_ref, local_ref, o_ref,
    q_ref, k_ref, v_ref, s_k, s_v, s_q, s_ref, r_q, r_ref, s_epi_k, s_epi_v, r_epi_k, r_epi_v, s_out, r_out,
    both_k, both_v, cands, cross, r_cross, k_own, v_own, k_epi, v_epi, q_two, acc, top, scores, send_table,
    sem_k, sem_v, sem_q, sem_ref, sem_epi_k, sem_epi_v, sem_out, sem_hop, sem_in,
):
    tm, tok = lax.axis_index("tm"), lax.axis_index("tok")
    core, pair = lax.rem(tm, 2), lax.rem(tm // 2, 2)
    partner, across = tm + 1 - 2 * core, tm + 2 - 4 * pair
    group = tm // SPAN

    def other(me, step):
        return lax.rem(me + step, N)

    def rest(fn):
        lax.fori_loop(1, N, lambda step, _: (fn(step), 0)[1], 0)

    def copy(src, dst, sems, sent, got, axis, to):
        return pltpu.make_async_remote_copy(
            src_ref=src, dst_ref=dst, send_sem=sems.at[0, sent], recv_sem=sems.at[1, got],
            device_id={axis: to}, device_id_type=MESH,
        )

    class Exchange:
        def __init__(self, src, dst, sems, axis):
            self.src, self.dst, self.sems, self.axis = src, dst, sems, axis
            self.me = tm if axis == "tm" else tok

        def to(self, peer):
            return copy(self.src.at[peer], self.dst.at[self.me], self.sems, peer, self.me, self.axis, peer)

        def start(self):
            if self.axis == "tm":
                rest(lambda step: self.to(other(self.me, step)).start())
                return
            row, column = self.me // SIDE, lax.rem(self.me, SIDE)
            for dx, dy in FAR_FIRST:
                self.to(lax.rem(row + dx, SIDE) * SIDE + lax.rem(column + dy, SIDE)).start()

        def keep(self):
            self.dst[self.me] = self.src[self.me]

        def arrive(self):
            def one(step):
                peer = other(self.me, step)
                copy(self.src.at[peer], self.dst.at[peer], self.sems, peer, peer, self.axis, peer).wait_recv()

            rest(one)

        def drain(self):
            rest(lambda step: self.to(other(self.me, step)).wait_send())

    r_k, r_v = both_k.at[0], both_v.at[0]
    swap_k, swap_v = Exchange(s_k, r_k, sem_k, "tok"), Exchange(s_v, r_v, sem_v, "tok")
    swap_q, swap_ref = Exchange(s_q, r_q, sem_q, "tok"), Exchange(s_ref, r_ref, sem_ref, "tok")
    epi_k, epi_v = Exchange(s_epi_k, r_epi_k, sem_epi_k, "tm"), Exchange(s_epi_v, r_epi_v, sem_epi_v, "tm")
    outs = Exchange(s_out, r_out, sem_out, "tok")

    barrier = pltpu.get_barrier_semaphore()

    def greet(step):
        pl.semaphore_signal(barrier, inc=1, device_id={"tok": other(tok, step)}, device_id_type=MESH)
        pl.semaphore_signal(barrier, inc=1, device_id={"tm": other(tm, step)}, device_id_type=MESH)

    fetches = [
        pltpu.make_async_copy(src, dst, sem_in.at[i])
        for i, (src, dst) in enumerate(((k_hbm, k_ref), (v_hbm, v_ref), (q_hbm, q_ref)))
    ]
    for fetch in fetches:
        fetch.start()
    rest(greet)

    def pack(ref, out):
        for j in range(HEADS // 2):
            lanes = slice(j * 128, (j + 1) * 128)
            a, b = ref[0, :, lanes], ref[1, :, lanes]
            out[2 * j] = low_halves(a, b)
            out[2 * j + 1] = high_halves(a, b)

    for fetch, ref, out in zip(fetches, (k_ref, v_ref, q_ref), (s_k, s_v, s_q)):
        fetch.wait()
        pack(ref, out)
    local = local_ref[group]
    owner_core, owner_pair, ref_bit = lax.rem(local // 2, 2), local // 4, lax.rem(local, 2)
    for j in range(HEADS // 2):
        lanes = slice(j * 128, (j + 1) * 128)
        a, b = k_ref[ref_bit, :, lanes], v_ref[ref_bit, :, lanes]
        cands[core, 2 * j] = low_halves(a, b)
        cands[core, 2 * j + 1] = high_halves(a, b)

    pl.semaphore_wait(barrier, 2 * (N - 1))
    swap = copy(cands.at[core], cands.at[core], sem_hop, 0, 0, "tm", partner)
    swap.start()
    for exchange in (swap_k, swap_v, swap_q):
        exchange.start()
    for exchange in (swap_k, swap_v, swap_q):
        exchange.keep()

    part = N // 2
    mine, theirs = pl.ds(core * part, part), pl.ds((1 - core) * part, part)
    swap.wait_recv()
    cross[...] = cands[owner_core, mine]
    hop = copy(cross, r_cross.at[mine], sem_hop, 1, 1, "tm", across)
    hop.start()

    def fill_send(d, _):
        for f in range(FRAMES_DEV):
            row, place = d * FRAMES_DEV + f, jnp.int32(0)
            for e in range(ENTRIES):
                spot = block_ref[e, row] * 2 + frame_ref[e, row]
                place = jnp.where(dev_ref[e, row] == tm, spot, place)
            send_table[d * 2 + f] = place
        return 0

    lax.fori_loop(0, N, fill_send, 0)

    acc[...] = jnp.zeros_like(acc)
    top[...] = jnp.full_like(top, -1e30)
    for f in range(3):
        v_own[f, 0:16, :] = jnp.ones((16, TOKENS), BF16)

    low = lax.broadcasted_iota(jnp.int32, (BLOCK, 128), 1) < HEAD_DIM

    def over_blocks(fn):
        def one(b, _):
            fn(b, pl.ds(pl.multiple_of(b * BLOCK, BLOCK), BLOCK))
            return 0

        lax.fori_loop(0, N, one, 0, unroll=4)

    def fill_epi(both, s_epi):
        def one(d, _):
            first, second = send_table[d * 2], send_table[d * 2 + 1]
            a, b = both[lax.rem(first, 2), first // 2], both[1 - lax.rem(second, 2), second // 2]
            s_epi[d] = jnp.where(low, a, b)
            return 0

        lax.fori_loop(0, N, one, 0, unroll=4)

    swap_k.arrive()

    def build_k(b, at):
        x = both_k[0, b]
        y = jnp.concatenate([x[:, HEAD_DIM:], x[:, :HEAD_DIM]], axis=1)
        both_k[1, b] = y
        k_own[0, at, :] = jnp.where(low, x, y)
        k_own[1, at, :] = jnp.where(low, y, x)

    over_blocks(build_k)
    fill_epi(both_k, s_epi_k)
    epi_k.start()
    epi_k.keep()

    hop.wait_recv()
    swap_back = copy(r_cross.at[mine], r_cross.at[mine], sem_hop, 2, 2, "tm", partner)
    swap_in = copy(r_cross.at[theirs], r_cross.at[theirs], sem_hop, 2, 2, "tm", partner)
    swap_back.start()

    swap_v.arrive()

    def build_v(b, at):
        x = both_v[0, b]
        both_v[1, b] = jnp.concatenate([x[:, HEAD_DIM:], x[:, :HEAD_DIM]], axis=1)
        x = x.T
        v_own[0, 16:, at] = x[:HEAD_DIM]
        v_own[1, 16:, at] = x[HEAD_DIM:]

    over_blocks(build_v)
    fill_epi(both_v, s_epi_v)
    epi_v.start()
    epi_v.keep()

    swap_in.wait_recv()

    def pick_ref(b, at):
        s_ref[b] = jnp.where(owner_pair == pair, cands[owner_core, b], r_cross[b])

    over_blocks(pick_ref)
    swap_ref.start()
    swap_ref.keep()

    swap_q.arrive()

    def build_q(b, at):
        x = r_q[b].astype(F32) * QK_SCALE
        hi = x.astype(BF16)
        lo = (x - hi.astype(F32)).astype(BF16)
        q_two[0, at, :] = low_halves(hi, lo)
        q_two[1, at, :] = high_halves(hi, lo)

    over_blocks(build_q)

    def attend(work, keys, values):
        def score(i):
            f, column, c = work[i]
            rows = pl.ds(pl.multiple_of(column * COLUMN, COLUMN), COLUMN)
            s = lax.dot_general(
                keys(f)[c * CHUNK:(c + 1) * CHUNK, :], q_two[f, rows, :], (((1,), (1,)), ((), ())),
                preferred_element_type=F32,
            )
            scores[i % (DEPTH + 1)] = s
            return jnp.max(s.reshape(CHUNK // 8, 8, COLUMN), axis=0)

        peaks = {i: score(i) for i in range(DEPTH)}
        for i, (f, column, c) in enumerate(work):
            if i + DEPTH < len(work):
                peaks[i + DEPTH] = score(i + DEPTH)
            old = top[f, column]
            peak = jnp.max(peaks.pop(i), axis=0, keepdims=True)
            new = jnp.maximum(old, jnp.broadcast_to(peak, (8, COLUMN)))
            probs = jnp.exp2(scores[i % (DEPTH + 1)] - new[:1]).astype(BF16)
            part_sum = jnp.dot(values(f)[:, c * CHUNK:(c + 1) * CHUNK], probs, preferred_element_type=F32)
            acc[f, column] = acc[f, column] * jnp.exp2(old - new)[:1] + part_sum
            top[f, column] = new

    per_tile, columns = TILE // BLOCK, TILE // COLUMN

    def build_ref(b, at):
        kv = r_ref[b]
        k_own[2, at, :] = low_halves(kv, kv)
        v_own[2, 16:, at] = kv.T[HEAD_DIM:]

    def build_epi():
        for f in range(FRAMES_DEV):
            side = slice(f * HEAD_DIM, (f + 1) * HEAD_DIM)
            for e in range(ENTRIES):
                row, at = tm * FRAMES_DEV + f, slice(e * BLOCK, (e + 1) * BLOCK)
                source, used = dev_ref[e, row], valid_ref[e, row] > 0
                x = jnp.where(used, r_epi_k[source][:, side], r_k[0][:, side])
                k_epi[f, at, :] = jnp.concatenate([x, x], axis=1)
                weight = jnp.where(used, 1.0, 0.0).astype(F32)
                v_epi[f, 0:16, at] = jnp.full((16, BLOCK), weight, F32).astype(BF16)
                y = r_epi_v[source]
                v_epi[f, 16:, at] = jnp.where(used, y, jnp.zeros_like(y)).T[side]

    def long_step(n, _):
        @pl.when(n == 1)
        def _():
            swap_ref.arrive()
            over_blocks(build_ref)

        work = [
            (f, t, c)
            for f in range(FRAMES_DEV) for c in range(TOKENS // CHUNK) for t in range(TOKENS // COLUMN)
        ]

        def which(f):
            return jnp.where(n == 0, f, FRAMES_DEV)

        attend(work, lambda f: k_own.at[which(f)], lambda f: v_own.at[which(f)])
        return 0

    lax.fori_loop(0, 2, long_step, 0)
    epi_k.arrive()
    epi_v.arrive()
    build_epi()

    def short_step(n, _):
        tile = lax.rem(n + tok // per_tile, TILES)
        work = [
            (f, tile * columns + t, c)
            for f in range(FRAMES_DEV) for c in range(EPI // CHUNK) for t in range(columns)
        ]
        attend(work, lambda f: k_epi.at[f], lambda f: v_epi.at[f])
        for t in range(columns):
            both = [acc[f, tile * columns + t] for f in range(FRAMES_DEV)]
            both = jnp.concatenate([x[16:] / x[:1] for x in both], axis=0).astype(BF16).T
            s_out[pl.ds(tile * per_tile + t * (COLUMN // BLOCK), COLUMN // BLOCK)] = both.reshape(-1, BLOCK, 128)
        for b in range(per_tile):
            to = tile * per_tile + b

            @pl.when(to != tok)
            def _():
                outs.to(to).start()

        return 0

    lax.fori_loop(0, TILES, short_step, 0)
    outs.keep()
    for exchange in (swap_k, swap_v, swap_q, swap_ref, epi_k, epi_v):
        exchange.drain()
    swap.wait_send()
    hop.wait_send()
    swap_back.wait_send()
    outs.arrive()
    for j in range(HEADS // 2):
        lanes = slice(j * 128, (j + 1) * 128)
        a, b = r_out[2 * j], r_out[2 * j + 1]
        o_ref[0, :, lanes] = low_halves(a, b)
        o_ref[1, :, lanes] = high_halves(a, b)
    outs.drain()


def attention(queries, keys, values, epi_dev, epi_frame, epi_block, valid, ref_local):
    vmem, smem = pl.BlockSpec(memory_space=pltpu.VMEM), pl.BlockSpec(memory_space=pltpu.SMEM)
    blocks = pltpu.VMEM((N, BLOCK, 128), BF16)
    tables = [x.T for x in (epi_dev, epi_frame, epi_block, valid)]
    return pl.pallas_call(
        kernel,
        out_shape=jax.ShapeDtypeStruct(queries.shape, BF16),
        in_specs=[pl.BlockSpec(memory_space=pl.ANY)] * 3 + [smem] * 5,
        out_specs=vmem,
        scratch_shapes=[
            *[pltpu.VMEM(queries.shape, BF16)] * 3,
            *[blocks] * 12,
            *[pltpu.VMEM((2, N, BLOCK, 128), BF16)] * 2,
            pltpu.VMEM((2, N, BLOCK, 128), BF16),
            pltpu.VMEM((N // 2, BLOCK, 128), BF16),
            blocks,
            pltpu.VMEM((3, TOKENS, 128), BF16),
            pltpu.VMEM((3, ROWS, TOKENS), BF16),
            pltpu.VMEM((FRAMES_DEV, EPI, 128), BF16),
            pltpu.VMEM((FRAMES_DEV, ROWS, EPI), BF16),
            pltpu.VMEM((FRAMES_DEV, TOKENS, 128), BF16),
            pltpu.VMEM((FRAMES_DEV, TOKENS // COLUMN, ROWS, COLUMN), F32),
            pltpu.VMEM((FRAMES_DEV, TOKENS // COLUMN, 8, COLUMN), F32),
            pltpu.VMEM((DEPTH + 1, CHUNK, COLUMN), F32),
            pltpu.SMEM((2 * N,), jnp.int32),
            *[pltpu.SemaphoreType.DMA((2, N))] * 7,
            pltpu.SemaphoreType.DMA((2, 3)),
            pltpu.SemaphoreType.DMA((3,)),
        ],
        compiler_params=pltpu.CompilerParams(
            collective_id=0, has_side_effects=True, vmem_limit_bytes=60 * 2**20
        ),
    )(queries, keys, values, *tables, ref_local)


def solution(mesh):
    shard = P("tm", "tok", None)
    return jax.shard_map(
        attention,
        mesh=mesh,
        in_specs=(shard, shard, shard, P(), P(), P(), P(), P()),
        out_specs=shard,
        check_vma=False,
    )
```
